32 devices in a mesh: pair: 4 (over x, core), pw: 8 (over z, y).
Axes of the slice: x: 2, y: 2, z: 4, core: 2. Of those that a mesh axis runs over, the one named last changes fastest.
Arguments:
- pair_products: bfloat16 [32768, 2048], P('pw', 'pair'), may hold values from -40 to 40
- basis: bfloat16 [32768, 1024], P('pw'), may hold values from -0.046875 to 0.046875
- val_energy: float32 [128], replicated, may hold values from -0.05 to -0.001
- cond_energy: float32 [128], replicated, may hold values from 0.001 to 40
- frequencies: float32 [8], replicated, may hold values from 0.002 to 20
- valence_index: int32 [2048], P('pair'), may hold values from 0 to 127
- conduction_index: int32 [2048], P('pair'), may hold values from 0 to 127
Outputs:
- response: float32 [8, 1024, 1024], P(None, 'pw', 'pair')
The draws below stay inside these ranges and needn't reach their ends.
All inputs are finite; a program needn't handle non-finite values.
Results may differ from the reference program's by a relative error of at most 0.0055.
Values may be sent and summed in bfloat16 or wider, within the bound.
No kernel may reach another device: no remote copies, remote signals or barrier semaphores. Data moves between devices by JAX's collectives and lax.ppermute only.
A program may use at most 64 MiB of HBM per device.

```python
import math
import jax
import jax.numpy as jnp
from jax import lax

NPW = 32768
NB = 1024
NW = 8
NV = 128
NC = 128
GROUPS = 2
PAIRS = 2048
N_PAIR = 4


def band_tables(key):
    valence = jax.random.randint(jax.random.fold_in(key, 101), (PAIRS,), 0, NV).astype(jnp.int32)
    conduction = jax.random.randint(jax.random.fold_in(key, 102), (PAIRS,), 0, NC).astype(jnp.int32)
    depths = jnp.exp(jax.random.uniform(jax.random.fold_in(key, 103), (NV,), jnp.float32, math.log(0.001), math.log(0.05)))
    heights = jnp.exp(jax.random.uniform(jax.random.fold_in(key, 104), (NC,), jnp.float32, math.log(0.001), math.log(40.0)))
    lower = -jnp.clip(depths, 0.001, 0.05)
    upper = jnp.clip(heights, 0.001, 40.0)
    return (valence, conduction, lower, upper)


def draw_valence_index(key, part):
    return band_tables(key)[0]


def draw_conduction_index(key, part):
    return band_tables(key)[1]


def draw_val_energy(key, part):
    return band_tables(key)[2]


def draw_cond_energy(key, part):
    return band_tables(key)[3]


def draw_pair_products(key, part):
    valence, conduction, lower, upper = band_tables(key)
    energy_gap = upper[conduction] - lower[valence]
    column_scale = jnp.sqrt(energy_gap)
    values = jnp.clip(jax.random.normal(jax.random.fold_in(key, 105), (NPW, PAIRS), jnp.float32), -6.0, 6.0)
    return jnp.clip(values * column_scale[None, :], -40.0, 40.0).astype(jnp.bfloat16)


def draw_frequencies(key, part):
    shifts = jax.random.uniform(jax.random.fold_in(key, 201), (NW,), jnp.float32, 0.1, 0.9)
    order = jax.random.permutation(jax.random.fold_in(key, 202), NW).astype(jnp.float32)
    low_end = math.log(0.002)
    high_end = math.log(20.0)
    levels = (order + shifts) * ((high_end - low_end) / NW) + low_end
    return jnp.clip(jnp.exp(levels), 0.002, 20.0)


def raised(result, own_key, source, target, parts, factor):
    owner, partner = [(jnp.arange(result.shape[dim]) // (result.shape[dim] // parts)).reshape([-1 if axis == dim else 1 for axis in range(result.ndim)]) for dim in (source, target)]
    chosen = jax.random.permutation(own_key, parts)[partner]
    strong = (owner == chosen) | (owner == (partner + parts // 2) % parts)
    return jnp.where(strong, factor * result, result)


def steps_of(rng, extent, split, least, high):
    loudness, own = 1.0, jax.random.fold_in(rng, 6)
    for dim, shards_of in split:
        steps = jnp.exp(jax.random.uniform(jax.random.fold_in(own, dim), (shards_of,), jnp.float32, least / len(split), high / len(split)))
        loudness = loudness * jnp.repeat(steps, extent[dim] // shards_of).reshape([-1 if axis == dim else 1 for axis in range(len(extent))])
    return loudness


def heavy_noise(own_key, extent, spread, reach, pieces, heavy, kind=jnp.bfloat16):
    drawn = spread * jax.random.normal(own_key, extent, jnp.float32)
    if pieces:
        drawn = drawn * steps_of(own_key, extent, pieces, -0.22, 0.18)
    return jnp.clip(raised(drawn, jax.random.fold_in(own_key, 3), *heavy), -reach, reach).astype(kind)


def setup_inputs(seed: int = 0) -> dict:
    splits = jax.random.split(jax.random.key(seed), 8)
    pair_products = draw_pair_products(jax.random.fold_in(splits[7], 71), 0)
    basis = heavy_noise(splits[1], (NPW, NB), NPW ** -0.5, 0.046875, ((0, 8),), (0, 1, 8, 2.0))
    val_energy = draw_val_energy(jax.random.fold_in(splits[7], 71), 0)
    cond_energy = draw_cond_energy(jax.random.fold_in(splits[7], 71), 0)
    frequencies = draw_frequencies(jax.random.fold_in(splits[7], 71), 0)
    valence_index = draw_valence_index(jax.random.fold_in(splits[7], 71), 0)
    conduction_index = draw_conduction_index(jax.random.fold_in(splits[7], 71), 0)
    return dict(pair_products=pair_products, basis=basis, val_energy=val_energy, cond_energy=cond_energy, frequencies=frequencies, valence_index=valence_index, conduction_index=conduction_index)


def reference(pair_products, basis, val_energy, cond_energy, frequencies, valence_index, conduction_index):
    energy_gap = cond_energy[conduction_index] - val_energy[valence_index]
    weights = -4.0 * energy_gap[None, :] / (energy_gap[None, :] ** 2 + frequencies[:, None] ** 2) / PAIRS
    block_size = PAIRS // (N_PAIR * GROUPS)

    def add_block(gram_total, position):
        offset = (position * block_size).astype(jnp.int32)
        pair_block = lax.dynamic_slice_in_dim(pair_products, offset, block_size, 1)
        projected = lax.dot_general(basis, pair_block, (((0,), (0,)), ((), ())), preferred_element_type=jnp.float32).astype(jnp.bfloat16)
        weight_block = lax.dynamic_slice_in_dim(weights, offset, block_size, 1)
        weighted = (weight_block[:, None, :] * projected.astype(jnp.float32)[None]).astype(jnp.bfloat16)
        gram_total = gram_total + jnp.einsum("kpc,nc->kpn", weighted.astype(jnp.float32), projected.astype(jnp.float32))
        return gram_total, None

    start_total = jnp.zeros((NW, NB, NB), jnp.float32)
    response, _ = lax.scan(add_block, start_total, jnp.arange(N_PAIR * GROUPS, dtype=jnp.int32))
    return response
```

```python
import jax
import jax.numpy as jnp
from jax import lax
from jax.sharding import PartitionSpec as P

GROUPS = 2
GAP_ROWS = 16


def lookup(index_array, table):
    levels = lax.broadcasted_iota(jnp.int32, (index_array.shape[0], table.shape[0]), 1)
    return jnp.sum(jnp.where(index_array[:, None] == levels, table[None, :], 0.0), axis=1)


def flip(size, mask):
    return [(i, i ^ mask) for i in range(size)]


def split_gap(gap):
    parts = []
    left = gap
    for _ in range(3):
        part = lax.reduce_precision(left, 8, 7)
        parts.append(part.astype(jnp.bfloat16))
        left = left - part
    rows = jnp.stack(parts)
    return jnp.pad(rows, ((0, GAP_ROWS - rows.shape[0]), (0, 0)))


def join_gap(rows):
    terms = rows[:3].astype(jnp.float32)
    return terms[0] + (terms[1] + terms[2])


def halves(blocks, bit, place):
    n, rows, cols = blocks.shape
    low = 1 << place
    view = blocks.reshape(n // (2 * low), 2, low, rows, cols)
    pick = lambda b: lax.dynamic_index_in_dim(view, b, 1, False).reshape(n // 2, rows, cols)
    return pick(bit), pick(1 - bit)


def merge(mine, other, bit, place):
    n, rows, cols = mine.shape
    low = 1 << place
    first = jnp.where(bit == 0, mine, other).reshape(n // low, 1, low, rows, cols)
    second = jnp.where(bit == 0, other, mine).reshape(n // low, 1, low, rows, cols)
    return jnp.concatenate([first, second], 1).reshape(2 * n, rows, cols)


def sum_low_bits(partial, order, n_pw, me):
    blocks = partial.reshape(n_pw, partial.shape[0] // n_pw, partial.shape[1])
    gone = []
    for number in order:
        place = number - sum(g < number for g in gone)
        kept, sent = halves(blocks, (me >> number) & 1, place)
        got = lax.ppermute(sent.astype(jnp.bfloat16), "pw", flip(n_pw, 1 << number))
        blocks = kept + got.astype(jnp.float32)
        gone.append(number)
    got = lax.ppermute(blocks.astype(jnp.bfloat16), "pw", flip(n_pw, n_pw // 2))
    return (blocks + got.astype(jnp.float32)).astype(jnp.bfloat16)


def exchange(summed, gap_rows, order, n_pair, n_pw, j, me):
    blocks = summed
    left = sorted(order)
    gone = list(order)
    for number in reversed(order):
        gone.remove(number)
        place = number - sum(g < number for g in gone)
        got = lax.ppermute(blocks, "pw", flip(n_pw, 1 << number))
        blocks = merge(blocks, got, (me >> number) & 1, place)
    n, rows, cols = blocks.shape
    own = lax.dynamic_index_in_dim(blocks, me, 0, False)
    tiles = blocks.reshape(n_pair, n * rows // n_pair, cols)
    parts = []
    for d in range(n_pair):
        tile = lax.dynamic_index_in_dim(tiles, j ^ d, 0, False)
        piece = jnp.concatenate([tile, own, gap_rows], 0)
        parts.append(lax.ppermute(piece, "pair", flip(n_pair, d)) if d else piece)
    whole = jnp.concatenate(parts, 1)
    m_rows = tiles.shape[1]
    return whole[m_rows : m_rows + rows], whole[:m_rows], join_gap(whole[m_rows + rows :])


def per_device(
    pair_products, basis, val_energy, cond_energy, frequencies, valence_index, conduction_index
):
    n_pair, n_pw = lax.axis_size("pair"), lax.axis_size("pw")
    j, me = lax.axis_index("pair"), lax.axis_index("pw")
    bits = n_pw.bit_length() - 1
    rows_local = pair_products.shape[1]
    pairs_total = rows_local * n_pair
    block_size = rows_local // GROUPS
    gap = lookup(conduction_index, cond_energy) - lookup(valence_index, val_energy)
    total = None
    for group in range(GROUPS):
        cut = slice(group * block_size, (group + 1) * block_size)
        order = list(range(bits - 1))
        if group % 2:
            order[:2] = order[:2][::-1]
        partial = lax.dot_general(
            basis, pair_products[:, cut], (((0,), (0,)), ((), ())),
            preferred_element_type=jnp.float32,
        )
        summed = sum_low_bits(partial, order, n_pw, me)
        rows_n, rows_m, gaps = exchange(summed, split_gap(gap[cut]), order, n_pair, n_pw, j, me)
        weights = (
            -4.0 * gaps[None, :] / (gaps[None, :] ** 2 + frequencies[:, None] ** 2) / pairs_total
        )
        weighted = (weights[:, None, :] * rows_n.astype(jnp.float32)[None]).astype(jnp.bfloat16)
        part = jnp.einsum("kpc,nc->kpn", weighted, rows_m, preferred_element_type=jnp.float32)
        total = part if total is None else total + part
    return total


def solution(mesh):
    placed = (P("pw", "pair"), P("pw", None), P(), P(), P(), P("pair"), P("pair"))
    return jax.shard_map(
        per_device, mesh=mesh, in_specs=placed, out_specs=P(None, "pw", "pair"), check_vma=False
    )
```

```python
import jax
import jax.numpy as jnp
from jax import lax
from jax.experimental import pallas as pl
from jax.experimental.pallas import tpu as pltpu
from jax.sharding import PartitionSpec as P

GROUPS = 2
LOADS = 8
GAP_ROWS = 16


def lookup(index_array, table):
    levels = lax.broadcasted_iota(jnp.int32, (index_array.shape[0], table.shape[0]), 1)
    return jnp.sum(jnp.where(index_array[:, None] == levels, table[None, :], 0.0), axis=1)


def flip(size, mask):
    return [(i, i ^ mask) for i in range(size)]


def split_gap(gap):
    parts = []
    left = gap
    for _ in range(3):
        part = lax.reduce_precision(left, 8, 7)
        parts.append(part.astype(jnp.bfloat16))
        left = left - part
    rows = jnp.stack(parts)
    return jnp.pad(rows, ((0, GAP_ROWS - rows.shape[0]), (0, 0)))


def join_gap(rows):
    terms = rows[:3].astype(jnp.float32)
    return terms[0] + (terms[1] + terms[2])


def halves(blocks, bit, place):
    n, rows, cols = blocks.shape
    low = 1 << place
    view = blocks.reshape(n // (2 * low), 2, low, rows, cols)
    pick = lambda b: lax.dynamic_index_in_dim(view, b, 1, False).reshape(n // 2, rows, cols)
    return pick(bit), pick(1 - bit)


def merge(mine, other, bit, place):
    n, rows, cols = mine.shape
    low = 1 << place
    first = jnp.where(bit == 0, mine, other).reshape(n // low, 1, low, rows, cols)
    second = jnp.where(bit == 0, other, mine).reshape(n // low, 1, low, rows, cols)
    return jnp.concatenate([first, second], 1).reshape(2 * n, rows, cols)


def with_bit(index, bit, place):
    return ((index >> place) << (place + 1)) | (bit << place) | (index & ((1 << place) - 1))


def project_body(me_ref, basis_ref, pairs_ref, *refs, firsts, n_pw):
    outs = refs[: 2 * len(firsts)]
    basis_mem, pairs_mem, acc, sems = refs[2 * len(firsts) :]
    step = basis_mem.shape[0] // LOADS
    spans = [pl.ds(n * step, step) for n in range(LOADS)]
    copies = [
        [
            pltpu.make_async_copy(basis_ref.at[span], basis_mem.at[span], sems.at[0, n]),
            pltpu.make_async_copy(pairs_ref.at[span], pairs_mem.at[span], sems.at[1, n]),
        ]
        for n, span in enumerate(spans)
    ]
    for both in copies:
        for copy in both:
            copy.start()
    for n, span in enumerate(spans):
        for copy in copies[n]:
            copy.wait()
        product = lax.dot_general(
            basis_mem[span], pairs_mem[span], (((0,), (0,)), ((), ())),
            preferred_element_type=jnp.float32,
        )
        acc[...] = product if n == 0 else acc[...] + product
    rows = acc.shape[0] // n_pw
    cols = acc.shape[1] // len(firsts)
    for group, first in enumerate(firsts):
        kept_ref, sent_ref = outs[2 * group], outs[2 * group + 1]
        span = pl.ds(group * cols, cols)
        bit = (me_ref[0] >> first) & 1
        for q in range(n_pw // 2):
            mine = pl.multiple_of(with_bit(q, bit, first) * rows, rows)
            other = pl.multiple_of(with_bit(q, 1 - bit, first) * rows, rows)
            kept_ref[q] = acc[pl.ds(mine, rows), span]
            sent_ref[q] = acc[pl.ds(other, rows), span].astype(jnp.bfloat16)


def project(basis, pair_products, me, firsts, n_pw):
    depth, rows_all = basis.shape
    cols_all = pair_products.shape[1]
    shape = (n_pw // 2, rows_all // n_pw, cols_all // len(firsts))
    outs = []
    for _ in firsts:
        outs += [jax.ShapeDtypeStruct(shape, jnp.float32), jax.ShapeDtypeStruct(shape, jnp.bfloat16)]
    body = lambda *refs: project_body(*refs, firsts=firsts, n_pw=n_pw)
    flat = pl.pallas_call(
        body,
        in_specs=[
            pl.BlockSpec(memory_space=pltpu.SMEM),
            pl.BlockSpec(memory_space=pl.ANY),
            pl.BlockSpec(memory_space=pl.ANY),
        ],
        out_shape=outs,
        scratch_shapes=[
            pltpu.VMEM(basis.shape, basis.dtype),
            pltpu.VMEM(pair_products.shape, pair_products.dtype),
            pltpu.VMEM((rows_all, cols_all), jnp.float32),
            pltpu.SemaphoreType.DMA((2, LOADS)),
        ],
        name="project",
    )(me.astype(jnp.int32)[None], basis, pair_products)
    return [(flat[2 * g], flat[2 * g + 1]) for g in range(len(firsts))]


def sum_low_bits(kept, sent, order, n_pw, me):
    gone = []
    for number in order:
        place = number - sum(g < number for g in gone)
        if gone:
            kept, sent = halves(blocks, (me >> number) & 1, place)
        got = lax.ppermute(sent.astype(jnp.bfloat16), "pw", flip(n_pw, 1 << number))
        blocks = kept + got.astype(jnp.float32)
        gone.append(number)
    got = lax.ppermute(blocks.astype(jnp.bfloat16), "pw", flip(n_pw, n_pw // 2))
    return (blocks + got.astype(jnp.float32)).astype(jnp.bfloat16)


def exchange(summed, gap_rows, order, n_pair, n_pw, j, me):
    blocks = summed
    left = sorted(order)
    gone = list(order)
    for number in reversed(order):
        gone.remove(number)
        place = number - sum(g < number for g in gone)
        got = lax.ppermute(blocks, "pw", flip(n_pw, 1 << number))
        blocks = merge(blocks, got, (me >> number) & 1, place)
    n, rows, cols = blocks.shape
    own = lax.dynamic_index_in_dim(blocks, me, 0, False)
    tiles = blocks.reshape(n_pair, n * rows // n_pair, cols)
    parts = []
    for d in range(n_pair):
        tile = lax.dynamic_index_in_dim(tiles, j ^ d, 0, False)
        piece = jnp.concatenate([tile, own, gap_rows], 0)
        parts.append(lax.ppermute(piece, "pair", flip(n_pair, d)) if d else piece)
    whole = jnp.concatenate(parts, 1)
    m_rows = tiles.shape[1]
    return whole[m_rows : m_rows + rows], whole[:m_rows], join_gap(whole[m_rows + rows :])


def exchange_square(summed, gap_rows, n_pair, n_pw, j, me):
    chip, core = j >> 1, j & 1
    far, near, side = me >> 2, (me >> 1) & 1, me & 1
    n, rows, cols = summed.shape
    own = jnp.concatenate([summed.reshape(n * rows, cols), gap_rows], 0)
    across = lax.ppermute(own, "pair", flip(n_pair, 2))
    both = jnp.concatenate([own, across], 1)
    twin = lax.ppermute(both, "pair", flip(n_pair, 1))
    whole = jnp.concatenate(
        [jnp.where(core == 0, both, twin), jnp.where(core == 0, twin, both)], 1
    )
    blocks = whole[: n * rows].reshape(n, rows, 2 * both.shape[1])
    rows_n = lax.dynamic_index_in_dim(blocks, far, 0, False)
    mine = lax.dynamic_index_in_dim(blocks, chip, 0, False)
    hop, diagonal = [], []
    for a in range(n_pair):
        for b in range(n_pw):
            if (a & 1) == (b >> 1) & 1:
                hop.append((a * n_pw + b, a * n_pw + (b ^ 1)))
                diagonal.append((a * n_pw + b, a * n_pw + (b ^ 3)))
            else:
                hop.append((a * n_pw + b, (a ^ 1) * n_pw + (b ^ 2)))
    first = lax.ppermute(mine, ("pair", "pw"), hop)
    second = lax.ppermute(mine, ("pair", "pw"), diagonal)
    here = core == near
    same = jnp.where(here, mine, first)
    other = jnp.where(here, first, second)
    rows_m = jnp.concatenate(
        [jnp.where(side == 0, same, other), jnp.where(side == 0, other, same)], 0
    )
    return rows_n, rows_m, join_gap(whole[n * rows :])


def per_device(
    pair_products, basis, val_energy, cond_energy, frequencies, valence_index, conduction_index
):
    n_pair, n_pw = lax.axis_size("pair"), lax.axis_size("pw")
    j, me = lax.axis_index("pair"), lax.axis_index("pw")
    bits = n_pw.bit_length() - 1
    rows_local = pair_products.shape[1]
    pairs_total = rows_local * n_pair
    block_size = rows_local // GROUPS
    gap = lookup(conduction_index, cond_energy) - lookup(valence_index, val_energy)
    total = None
    orders = []
    for group in range(GROUPS):
        order = list(range(bits - 1))
        if group % 2:
            order[:2] = order[:2][::-1]
        orders.append(order)
    partials = project(basis, pair_products, me, [order[0] for order in orders], n_pw)
    for group, order in enumerate(orders):
        cut = slice(group * block_size, (group + 1) * block_size)
        summed = sum_low_bits(*partials[group], order, n_pw, me)
        gap_rows = split_gap(gap[cut])
        if n_pair.bit_length() == 3 and n_pw.bit_length() == 4:
            rows_n, rows_m, gaps = exchange_square(summed, gap_rows, n_pair, n_pw, j, me)
        else:
            rows_n, rows_m, gaps = exchange(summed, gap_rows, order, n_pair, n_pw, j, me)
        weights = (
            -4.0 * gaps[None, :] / (gaps[None, :] ** 2 + frequencies[:, None] ** 2) / pairs_total
        )
        weighted = (weights[:, None, :] * rows_n.astype(jnp.float32)[None]).astype(jnp.bfloat16)
        part = jnp.einsum("kpc,nc->kpn", weighted, rows_m, preferred_element_type=jnp.float32)
        total = part if total is None else total + part
    return total


def solution(mesh):
    placed = (P("pw", "pair"), P("pw", None), P(), P(), P(), P("pair"), P("pair"))
    return jax.shard_map(
        per_device, mesh=mesh, in_specs=placed, out_specs=P(None, "pw", "pair"), check_vma=False
    )
```

```python
import jax
import jax.numpy as jnp
from jax import lax
from jax.experimental import pallas as pl
from jax.experimental.pallas import tpu as pltpu
from jax.sharding import PartitionSpec as P


GROUPS = 2
LOADS = 8
AHEAD = 3
VMEM_LIMIT = 24 << 20
GAP_ROWS = 16


def lookup(index_array, table):
    levels = lax.broadcasted_iota(jnp.int32, (index_array.shape[0], table.shape[0]), 1)
    return jnp.sum(jnp.where(index_array[:, None] == levels, table[None, :], 0.0), axis=1)


def flip(size, mask):
    return [(i, i ^ mask) for i in range(size)]


def split_gap(gap):
    parts = []
    left = gap
    for _ in range(3):
        part = lax.reduce_precision(left, 8, 7)
        parts.append(part.astype(jnp.bfloat16))
        left = left - part
    rows = jnp.stack(parts)
    return jnp.pad(rows, ((0, GAP_ROWS - rows.shape[0]), (0, 0)))


def join_gap(rows):
    terms = rows[:3].astype(jnp.float32)
    return terms[0] + (terms[1] + terms[2])


def halves(blocks, bit, place):
    n, rows, cols = blocks.shape
    low = 1 << place
    view = blocks.reshape(n // (2 * low), 2, low, rows, cols)
    pick = lambda b: lax.dynamic_index_in_dim(view, b, 1, False).reshape(n // 2, rows, cols)
    return pick(bit), pick(1 - bit)


def merge(mine, other, bit, place):
    n, rows, cols = mine.shape
    low = 1 << place
    first = jnp.where(bit == 0, mine, other).reshape(n // low, 1, low, rows, cols)
    second = jnp.where(bit == 0, other, mine).reshape(n // low, 1, low, rows, cols)
    return jnp.concatenate([first, second], 1).reshape(2 * n, rows, cols)


def with_bit(index, bit, place):
    return ((index >> place) << (place + 1)) | (bit << place) | (index & ((1 << place) - 1))


def project_body(me_ref, basis_ref, pairs_ref, kept_ref, sent_ref, *refs, group, first, n_pw):
    held = len(refs) == 1
    if held:
        (acc,) = refs
        basis_mem, pairs_mem = basis_ref, pairs_ref
    else:
        basis_mem, pairs_mem, acc, sems = refs
    step = basis_mem.shape[0] // LOADS
    spans = [pl.ds(n * step, step) for n in range(LOADS)]
    copies = [
        [
            pltpu.make_async_copy(source.at[span], target.at[span], sems.at[k, n])
            for k, (source, target) in enumerate([(basis_ref, basis_mem), (pairs_ref, pairs_mem)])
        ]
        for n, span in enumerate([] if held else spans)
    ]
    for copy in sum(copies[:AHEAD], []):
        copy.start()
    rows = acc.shape[0] // n_pw
    columns = pl.ds(group * acc.shape[1], acc.shape[1])
    for n, span in enumerate(spans):
        for copy in sum(copies[n : n + 1], []):
            copy.wait()
        for copy in sum(copies[n + AHEAD : n + AHEAD + 1], []):
            copy.start()
        product = lax.dot_general(
            basis_mem[span], pairs_mem[span, columns], (((0,), (0,)), ((), ())),
            preferred_element_type=jnp.float32,
        )
        acc[...] = product if n == 0 else acc[...] + product
    bit = (me_ref[0] >> first) & 1
    for q in range(n_pw // 2):
        mine = pl.multiple_of(with_bit(q, bit, first) * rows, rows)
        other = pl.multiple_of(with_bit(q, 1 - bit, first) * rows, rows)
        kept_ref[q] = acc[pl.ds(mine, rows)]
        sent_ref[q] = acc[pl.ds(other, rows)].astype(jnp.bfloat16)


def project(basis, pair_products, me, group, first, n_pw):
    _, rows_all = basis.shape
    cols = pair_products.shape[1] // GROUPS
    shape = (n_pw // 2, rows_all // n_pw, cols)
    outs = [pltpu.VMEM(shape, jnp.float32), pltpu.VMEM(shape, jnp.bfloat16)]
    scratch = [pltpu.VMEM((rows_all, cols), jnp.float32)]
    space = pltpu.VMEM if group else pltpu.HBM
    if not group:
        outs += [pltpu.VMEM(a.shape, a.dtype) for a in (basis, pair_products)]
        scratch.append(pltpu.SemaphoreType.DMA((2, LOADS)))
        basis = pltpu.with_memory_space_constraint(basis, space)
        pair_products = pltpu.with_memory_space_constraint(pair_products, space)
    body = lambda *refs: project_body(*refs, group=group, first=first, n_pw=n_pw)
    return pl.pallas_call(
        body,
        in_specs=[pl.BlockSpec(memory_space=pltpu.SMEM)] + [pl.BlockSpec(memory_space=space)] * 2,
        out_shape=outs,
        out_specs=[pl.BlockSpec(memory_space=pltpu.VMEM)] * len(outs),
        scratch_shapes=scratch,
        compiler_params=pltpu.CompilerParams(vmem_limit_bytes=VMEM_LIMIT),
        name="project",
    )(me.astype(jnp.int32)[None], basis, pair_products)


def sum_low_bits(kept, sent, order, n_pw, me):
    gone = []
    for number in order:
        place = number - sum(g < number for g in gone)
        if gone:
            kept, sent = halves(blocks, (me >> number) & 1, place)
        sent = sent.astype(jnp.bfloat16)
        got = lax.ppermute(sent, "pw", flip(n_pw, 1 << number))
        blocks = kept + got.astype(jnp.float32)
        gone.append(number)
    sent = blocks.astype(jnp.bfloat16)
    got = lax.ppermute(sent, "pw", flip(n_pw, n_pw // 2))
    return (blocks + got.astype(jnp.float32)).astype(jnp.bfloat16)


def exchange(summed, gap_rows, order, n_pair, n_pw, j, me):
    blocks = summed
    gone = list(order)
    for number in reversed(order):
        gone.remove(number)
        place = number - sum(g < number for g in gone)
        got = lax.ppermute(blocks, "pw", flip(n_pw, 1 << number))
        blocks = merge(blocks, got, (me >> number) & 1, place)
    n, rows, cols = blocks.shape
    own = lax.dynamic_index_in_dim(blocks, me, 0, False)
    tiles = blocks.reshape(n_pair, n * rows // n_pair, cols)
    parts = []
    for d in range(n_pair):
        tile = lax.dynamic_index_in_dim(tiles, j ^ d, 0, False)
        piece = jnp.concatenate([tile, own, gap_rows], 0)
        parts.append(lax.ppermute(piece, "pair", flip(n_pair, d)) if d else piece)
    whole = jnp.concatenate(parts, 1)
    m_rows = tiles.shape[1]
    return whole[m_rows : m_rows + rows], whole[:m_rows], join_gap(whole[m_rows + rows :])


def is_square(n_pair, n_pw):
    return n_pair.bit_length() == 3 and n_pw.bit_length() == 4


def exchange_square(summed, gap_rows, n_pair, n_pw, j, me):
    chip, core = j >> 1, j & 1
    far, near, side = me >> 2, (me >> 1) & 1, me & 1
    n, rows, cols = summed.shape
    own = jnp.concatenate([summed.reshape(n * rows, cols), gap_rows], 0)
    across = lax.ppermute(own, "pair", flip(n_pair, 2))
    both = jnp.concatenate([own, across], 1)
    twin = lax.ppermute(both, "pair", flip(n_pair, 1))
    whole = jnp.concatenate([jnp.where(core == 0, both, twin), jnp.where(core == 0, twin, both)], 1)
    blocks = whole[: n * rows].reshape(n, rows, 2 * both.shape[1])
    rows_n = lax.dynamic_index_in_dim(blocks, far, 0, False)
    mine = lax.dynamic_index_in_dim(blocks, chip, 0, False)
    hop, diagonal = [], []
    for a in range(n_pair):
        for b in range(n_pw):
            if (a & 1) == (b >> 1) & 1:
                hop.append((a * n_pw + b, a * n_pw + (b ^ 1)))
                diagonal.append((a * n_pw + b, a * n_pw + (b ^ 3)))
            else:
                hop.append((a * n_pw + b, (a ^ 1) * n_pw + (b ^ 2)))
    first = lax.ppermute(mine, ("pair", "pw"), hop)
    second = lax.ppermute(mine, ("pair", "pw"), diagonal)
    here = core == near
    same = jnp.where(here, mine, first)
    other = jnp.where(here, first, second)
    rows_m = jnp.concatenate(
        [jnp.where(side == 0, same, other), jnp.where(side == 0, other, same)], 0
    )
    return rows_n, rows_m, join_gap(whole[n * rows :])


def per_device(
    pair_products, basis, val_energy, cond_energy, frequencies, valence_index, conduction_index
):
    n_pair, n_pw = lax.axis_size("pair"), lax.axis_size("pw")
    j, me = lax.axis_index("pair"), lax.axis_index("pw")
    bits = n_pw.bit_length() - 1
    rows_local = pair_products.shape[1]
    pairs_total = rows_local * n_pair
    block_size = rows_local // GROUPS
    gap = lookup(conduction_index, cond_energy) - lookup(valence_index, val_energy)
    total = None
    orders = []
    for group in range(GROUPS):
        order = list(range(bits - 1))
        if group % 2:
            order[:2] = order[:2][::-1]
        orders.append(order)
    partials = []
    for group, order in enumerate(orders):
        kept, sent, *held = project(basis, pair_products, me, group, order[0], n_pw)
        if held:
            basis, pair_products = held
        partials.append((kept, sent))
    for group, order in enumerate(orders):
        cut = slice(group * block_size, (group + 1) * block_size)
        summed = sum_low_bits(*partials[group], order, n_pw, me)
        gap_rows = split_gap(gap[cut])
        if is_square(n_pair, n_pw):
            rows_n, rows_m, gaps = exchange_square(summed, gap_rows, n_pair, n_pw, j, me)
        else:
            rows_n, rows_m, gaps = exchange(summed, gap_rows, order, n_pair, n_pw, j, me)
        weights = (
            -4.0 * gaps[None, :] / (gaps[None, :] ** 2 + frequencies[:, None] ** 2) / pairs_total
        )
        weighted = (weights[:, None, :] * rows_n.astype(jnp.float32)[None]).astype(jnp.bfloat16)
        part = jnp.einsum("kpc,nc->kpn", weighted, rows_m, preferred_element_type=jnp.float32)
        total = part if total is None else total + part
    return total


def solution(mesh):
    placed = (P("pw", "pair"), P("pw", None), P(), P(), P(), P("pair"), P("pair"))

    return jax.shard_map(
        per_device, mesh=mesh, in_specs=placed, out_specs=P(None, "pw", "pair"), check_vma=False
    )
```

```python
import jax
import jax.numpy as jnp
from jax import lax
from jax.experimental import pallas as pl
from jax.experimental.pallas import tpu as pltpu
from jax.sharding import PartitionSpec as P


GROUPS = 2
DIRECT = (0, 1)
LOADS = 8
AHEAD = 3
VMEM_LIMIT = 24 << 20
GAP_ROWS = 16


def lookup(index_array, table):
    levels = lax.broadcasted_iota(jnp.int32, (index_array.shape[0], table.shape[0]), 1)
    return jnp.sum(jnp.where(index_array[:, None] == levels, table[None, :], 0.0), axis=1)


def flip(size, mask):
    return [(i, i ^ mask) for i in range(size)]


def split_gap(gap):
    parts = []
    left = gap
    for _ in range(3):
        part = lax.reduce_precision(left, 8, 7)
        parts.append(part.astype(jnp.bfloat16))
        left = left - part
    rows = jnp.stack(parts)
    return jnp.pad(rows, ((0, GAP_ROWS - rows.shape[0]), (0, 0)))


def join_gap(rows):
    terms = rows[:3].astype(jnp.float32)
    return terms[0] + (terms[1] + terms[2])


def halves(blocks, bit, place):
    n, rows, cols = blocks.shape
    low = 1 << place
    view = blocks.reshape(n // (2 * low), 2, low, rows, cols)
    pick = lambda b: lax.dynamic_index_in_dim(view, b, 1, False).reshape(n // 2, rows, cols)
    return pick(bit), pick(1 - bit)


def merge(mine, other, bit, place):
    n, rows, cols = mine.shape
    low = 1 << place
    first = jnp.where(bit == 0, mine, other).reshape(n // low, 1, low, rows, cols)
    second = jnp.where(bit == 0, other, mine).reshape(n // low, 1, low, rows, cols)
    return jnp.concatenate([first, second], 1).reshape(2 * n, rows, cols)


def with_bit(index, bit, place):
    return ((index >> place) << (place + 1)) | (bit << place) | (index & ((1 << place) - 1))


def project_body(me_ref, basis_ref, pairs_ref, *refs, group, picks, n_pw):
    kept_ref, *sent_refs = refs[: len(picks)]
    refs = refs[len(picks) :]
    held = len(refs) == 1
    if held:
        (acc,) = refs
        basis_mem, pairs_mem = basis_ref, pairs_ref
    else:
        basis_mem, pairs_mem, acc, sems = refs
    step = basis_mem.shape[0] // LOADS
    spans = [pl.ds(n * step, step) for n in range(LOADS)]
    copies = [
        [
            pltpu.make_async_copy(source.at[span], target.at[span], sems.at[k, n])
            for k, (source, target) in enumerate([(basis_ref, basis_mem), (pairs_ref, pairs_mem)])
        ]
        for n, span in enumerate([] if held else spans)
    ]
    for copy in sum(copies[:AHEAD], []):
        copy.start()
    rows = acc.shape[0] // n_pw
    columns = pl.ds(group * acc.shape[1], acc.shape[1])
    for n, span in enumerate(spans):
        for copy in sum(copies[n : n + 1], []):
            copy.wait()
        for copy in sum(copies[n + AHEAD : n + AHEAD + 1], []):
            copy.start()
        product = lax.dot_general(
            basis_mem[span], pairs_mem[span, columns], (((0,), (0,)), ((), ())),
            preferred_element_type=jnp.float32,
        )
        acc[...] = product if n == 0 else acc[...] + product
    for q in range(kept_ref.shape[0]):
        for pick, out_ref in zip(picks, [kept_ref] + sent_refs):
            start = pl.multiple_of(pick(q, me_ref[0]) * rows, rows)
            out_ref[q] = acc[pl.ds(start, rows)].astype(out_ref.dtype)


def project(basis, pair_products, me, group, picks, left, n_pw):
    _, rows_all = basis.shape
    cols = pair_products.shape[1] // GROUPS
    shape = (left, rows_all // n_pw, cols)
    outs = [pltpu.VMEM(shape, jnp.bfloat16 if n else jnp.float32) for n in range(len(picks))]
    scratch = [pltpu.VMEM((rows_all, cols), jnp.float32)]
    space = pltpu.VMEM if group else pltpu.HBM
    if not group:
        outs += [pltpu.VMEM(a.shape, a.dtype) for a in (basis, pair_products)]
        scratch.append(pltpu.SemaphoreType.DMA((2, LOADS)))
        basis = pltpu.with_memory_space_constraint(basis, space)
        pair_products = pltpu.with_memory_space_constraint(pair_products, space)
    body = lambda *refs: project_body(*refs, group=group, picks=picks, n_pw=n_pw)
    return pl.pallas_call(
        body,
        in_specs=[pl.BlockSpec(memory_space=pltpu.SMEM)] + [pl.BlockSpec(memory_space=space)] * 2,
        out_shape=outs,
        out_specs=[pl.BlockSpec(memory_space=pltpu.VMEM)] * len(outs),
        scratch_shapes=scratch,
        compiler_params=pltpu.CompilerParams(vmem_limit_bytes=VMEM_LIMIT),
        name="project",
    )(me.astype(jnp.int32)[None], basis, pair_products)


def sum_low_bits(kept, sent, order, n_pw, me):
    gone = []
    for number in order:
        place = number - sum(g < number for g in gone)
        if gone:
            kept, sent = halves(blocks, (me >> number) & 1, place)
        sent = sent.astype(jnp.bfloat16)
        got = lax.ppermute(sent, "pw", flip(n_pw, 1 << number))
        blocks = kept + got.astype(jnp.float32)
        gone.append(number)
    sent = blocks.astype(jnp.bfloat16)
    got = lax.ppermute(sent, "pw", flip(n_pw, n_pw // 2))
    return (blocks + got.astype(jnp.float32)).astype(jnp.bfloat16)


def exchange(summed, gap_rows, order, n_pair, n_pw, j, me):
    blocks = summed
    gone = list(order)
    for number in reversed(order):
        gone.remove(number)
        place = number - sum(g < number for g in gone)
        got = lax.ppermute(blocks, "pw", flip(n_pw, 1 << number))
        blocks = merge(blocks, got, (me >> number) & 1, place)
    n, rows, cols = blocks.shape
    own = lax.dynamic_index_in_dim(blocks, me, 0, False)
    tiles = blocks.reshape(n_pair, n * rows // n_pair, cols)
    parts = []
    for d in range(n_pair):
        tile = lax.dynamic_index_in_dim(tiles, j ^ d, 0, False)
        piece = jnp.concatenate([tile, own, gap_rows], 0)
        parts.append(lax.ppermute(piece, "pair", flip(n_pair, d)) if d else piece)
    whole = jnp.concatenate(parts, 1)
    m_rows = tiles.shape[1]
    return whole[m_rows : m_rows + rows], whole[:m_rows], join_gap(whole[m_rows + rows :])


def sum_direct(kept, *sent, n_pw):
    blocks = kept
    for d, block in enumerate(sent, 1):
        got = lax.ppermute(block, "pw", flip(n_pw, d))
        blocks = blocks + got.astype(jnp.float32)
    sent = blocks.astype(jnp.bfloat16)
    got = lax.ppermute(sent, "pw", flip(n_pw, n_pw // 2))
    return (blocks + got.astype(jnp.float32)).astype(jnp.bfloat16)


def is_square(n_pair, n_pw):
    return n_pair.bit_length() == 3 and n_pw.bit_length() == 4


def exchange_square(summed, gap_rows, n_pair, n_pw, j, me):
    chip, core = j >> 1, j & 1
    far, near, side = me >> 2, (me >> 1) & 1, me & 1
    n, rows, cols = summed.shape
    own = jnp.concatenate([summed.reshape(n * rows, cols), gap_rows], 0)
    across = lax.ppermute(own, "pair", flip(n_pair, 2))
    both = jnp.concatenate([own, across], 1)
    twin = lax.ppermute(both, "pair", flip(n_pair, 1))
    whole = jnp.concatenate([jnp.where(core == 0, both, twin), jnp.where(core == 0, twin, both)], 1)
    blocks = whole[: n * rows].reshape(n, rows, 2 * both.shape[1])
    rows_n = lax.dynamic_index_in_dim(blocks, far, 0, False)
    mine = lax.dynamic_index_in_dim(blocks, chip, 0, False)
    hop, diagonal = [], []
    for a in range(n_pair):
        for b in range(n_pw):
            if (a & 1) == (b >> 1) & 1:
                hop.append((a * n_pw + b, a * n_pw + (b ^ 1)))
                diagonal.append((a * n_pw + b, a * n_pw + (b ^ 3)))
            else:
                hop.append((a * n_pw + b, (a ^ 1) * n_pw + (b ^ 2)))
                diagonal.append((a * n_pw + b, (a ^ 1) * n_pw + b))
    first = lax.ppermute(mine, ("pair", "pw"), hop)
    second = lax.ppermute(mine, ("pair", "pw"), diagonal)
    here = core == near
    same = jnp.where(here, mine, first)
    other = jnp.where(here, first, second)
    rows_m = jnp.concatenate(
        [jnp.where(side == 0, same, other), jnp.where(side == 0, other, same)], 0
    )
    return rows_n, rows_m, join_gap(whole[n * rows :])


def per_device(
    pair_products, basis, val_energy, cond_energy, frequencies, valence_index, conduction_index
):
    n_pair, n_pw = lax.axis_size("pair"), lax.axis_size("pw")
    j, me = lax.axis_index("pair"), lax.axis_index("pw")
    bits = n_pw.bit_length() - 1
    rows_local = pair_products.shape[1]
    pairs_total = rows_local * n_pair
    block_size = rows_local // GROUPS
    gap = lookup(conduction_index, cond_energy) - lookup(valence_index, val_energy)
    total = None
    orders = []
    for group in range(GROUPS):
        order = list(range(bits - 1))
        if group % 2:
            order[:2] = order[:2][::-1]
        orders.append(order)
    partials = []
    direct = DIRECT if is_square(n_pair, n_pw) else ()
    for group, order in enumerate(orders):
        if group in direct:
            low = n_pw // 2
            picks = [lambda q, i, d=d: q * low + ((i & (low - 1)) ^ d) for d in range(low)]
            left = 2
        else:
            picks = [
                lambda q, i, d=d, p=order[0]: with_bit(q, ((i >> p) & 1) ^ d, p)
                for d in range(2)
            ]
            left = n_pw // 2
        outs = project(basis, pair_products, me, group, picks, left, n_pw)
        partials.append(outs[: len(picks)])
        basis, pair_products = outs[len(picks) :] or (basis, pair_products)
    for group, order in enumerate(orders):
        cut = slice(group * block_size, (group + 1) * block_size)
        if group in direct:
            summed = sum_direct(*partials[group], n_pw=n_pw)
        else:
            summed = sum_low_bits(*partials[group], order, n_pw, me)
        gap_rows = split_gap(gap[cut])
        if is_square(n_pair, n_pw):
            rows_n, rows_m, gaps = exchange_square(summed, gap_rows, n_pair, n_pw, j, me)
        else:
            rows_n, rows_m, gaps = exchange(summed, gap_rows, order, n_pair, n_pw, j, me)
        weights = (
            -4.0 * gaps[None, :] / (gaps[None, :] ** 2 + frequencies[:, None] ** 2) / pairs_total
        )
        weighted = (weights[:, None, :] * rows_n.astype(jnp.float32)[None]).astype(jnp.bfloat16)
        part = jnp.einsum("kpc,nc->kpn", weighted, rows_m, preferred_element_type=jnp.float32)
        total = part if total is None else total + part
    return total


def solution(mesh):
    placed = (P("pw", "pair"), P("pw", None), P(), P(), P(), P("pair"), P("pair"))

    return jax.shard_map(
        per_device, mesh=mesh, in_specs=placed, out_specs=P(None, "pw", "pair"), check_vma=False
    )
```
